32 devices in a mesh: rep: 2 (over x), ep: 4 (over y, core), grp: 4 (over z).
Axes of the slice: x: 2, y: 2, z: 4, core: 2. Of those that a mesh axis runs over, the one named last changes fastest.
Arguments:
- tokens: bfloat16 [4096, 4096], P(('rep', 'ep'), 'grp'), parts along dimension 0, may hold values from -6 to 6
- proj_in: bfloat16 [1024, 4096], P('ep', 'grp'), may hold values from -0.09375 to 0.09375
- proj_out: bfloat16 [1024, 4096], P('ep', 'grp'), may hold values from -0.1875 to 0.1875
- expert_up: bfloat16 [16, 1024, 2688], P(('ep', 'grp')), may hold values from -0.1875 to 0.1875
- expert_down: bfloat16 [16, 2688, 1024], P(('ep', 'grp')), may hold values from -0.125 to 0.125
- expert_ids: int32 [4096, 6], P(('rep', 'ep')), parts along dimension 0, may hold values from 0 to 15, as said below
- weight_codes: int32 [4096, 6], P(('rep', 'ep')), parts along dimension 0, may hold values from 1 to 64
Outputs:
- mixed: bfloat16 [4096, 4096], P(('rep', 'ep'), 'grp'), parts along dimension 0
The draws below stay inside these ranges and needn't reach their ends.
There are 2 independent parts, one for each index of `rep`. The reference program is written for one: setup_inputs(seed, part) draws one part's arguments, and reference() takes and returns one part's arrays. A program takes and returns all parts, laid end to end along the dimension named above; an argument that names none is the same for every part. Nothing has to cross between parts.
Inputs may be any that keep to these rules, and one draw needn't show every extreme that they name: `expert_ids`: expert e belongs to group e % 4. Each token picks 6 distinct experts, two in each of 3 distinct groups. Within each aligned block of 128 tokens (the tokens of one device), every group is picked from by exactly 96 tokens, no expert is picked by more than 64 tokens, and in every block each group has an expert picked by exactly 64.
All inputs are finite; a program needn't handle non-finite values.
Results may differ from the reference program's by a relative error of at most 0.012.
Values may be sent and summed in bfloat16 or wider, within the bound.
A program may use at most 64 MiB of HBM per device.

```python
import jax
import jax.numpy as jnp
from jax import lax

D = 4096
L = 1024
FF = 2688
GROUP_HITS = 3
PICKS = 6
TOK_DEV = 128
EXPERTS = 16
MOST = 64
TOKENS = 2048
N_EP = 4
N_GRP = 4


def group_labels(key):
    key_order, key_slots = jax.random.split(key)
    group_rows = TOK_DEV * GROUP_HITS // N_GRP
    order = jax.random.permutation(key_order, jnp.arange(N_EP, dtype=jnp.int32))
    rest = 2 * group_rows - MOST
    base = rest // (N_EP - 1)
    extra = rest % (N_EP - 1)
    ranks = jnp.arange(N_EP, dtype=jnp.int32)
    counts = jnp.where(ranks == 0, MOST, base + (ranks - 1 < extra).astype(jnp.int32)).astype(jnp.int32)
    labels = jnp.repeat(order, counts, total_repeat_length=2 * group_rows)
    slot_perm = jax.random.permutation(key_slots, jnp.arange(group_rows, dtype=jnp.int32))
    return (labels, slot_perm)


def block_ids(key):
    key_start, key_groups = jax.random.split(key)
    group_rows = TOK_DEV * GROUP_HITS // N_GRP
    starts = jax.random.permutation(key_start, jnp.arange(TOK_DEV, dtype=jnp.int32) % N_GRP)
    groups = (starts[:, None] + jnp.arange(GROUP_HITS, dtype=jnp.int32)[None, :]) % N_GRP
    hit = jnp.any(groups[:, :, None] == jnp.arange(N_GRP, dtype=jnp.int32), axis=1).astype(jnp.int32)
    rank_all = jnp.cumsum(hit, axis=0) - hit
    rank = jnp.take_along_axis(rank_all, groups, axis=1)
    labels, slot_perm = jax.vmap(group_labels)(jax.random.split(key_groups, N_GRP))
    slot = slot_perm[groups, rank]
    first = labels[groups, slot]
    second = labels[groups, slot + group_rows]
    members = jnp.stack([first, second], axis=2)
    ids = members * N_GRP + groups[:, :, None]
    return ids.reshape(TOK_DEV, 2 * GROUP_HITS).astype(jnp.int32)


def draw_expert_ids(key, part):
    blocks = TOKENS // TOK_DEV
    keys = jax.random.split(jax.random.fold_in(key, 7), blocks)
    return jax.vmap(block_ids)(keys).reshape(TOKENS, PICKS)


def plant(values, own_key, low, largest):
    longest = values.shape.index(max(values.shape))
    spots = []
    for shift in (0, 1):
        where = [jax.random.randint(jax.random.fold_in(own_key, axis), (), 0, length) for axis, length in enumerate(values.shape)]
        where[longest] = (where[longest] + shift) % values.shape[longest]
        spots.append(tuple(where))
    return values.at[spots[0]].set(low).at[spots[1]].set(largest)


def shard_levels(stream_key, dims, cuts, smallest, largest):
    level, own = 1.0, jax.random.fold_in(stream_key, 6)
    for position, shards_of in cuts:
        steps = jnp.exp(jax.random.uniform(jax.random.fold_in(own, position), (shards_of,), jnp.float32, smallest / len(cuts), largest / len(cuts)))
        level = level * jnp.repeat(steps, dims[position] // shards_of).reshape([-1 if axis == position else 1 for axis in range(len(dims))])
    return level


def gaussian(stream_key, shape, deviation, bound, cuts=(), kind=jnp.bfloat16):
    values = deviation * jax.random.normal(stream_key, shape, jnp.float32)
    if cuts:
        values = values * shard_levels(stream_key, shape, cuts, -0.22, 0.18)
    return jnp.clip(values, -bound, bound).astype(kind)


def setup_inputs(seed: int = 0, part: int = 0) -> dict:
    key_list = jax.random.split(jax.random.key(seed), 8)
    own_keys = jax.random.split(jax.random.fold_in(key_list[7], part), 8)
    return {
        "tokens": gaussian(own_keys[0], (TOKENS, D), 1.0, 6.0, ((0, 4), (1, 4))),
        "proj_in": gaussian(key_list[1], (L, D), D ** -0.5, 0.09375, ((0, 4), (1, 4))),
        "proj_out": gaussian(key_list[2], (L, D), L ** -0.5, 0.1875, ((0, 4), (1, 4))),
        "expert_up": gaussian(key_list[3], (EXPERTS, L, FF), L ** -0.5, 0.1875, ((0, 16),)),
        "expert_down": gaussian(key_list[4], (EXPERTS, FF, L), FF ** -0.5, 0.125, ((0, 16),)),
        "expert_ids": draw_expert_ids(jax.random.fold_in(jax.random.fold_in(key_list[7], part), 71), part),
        "weight_codes": plant(jax.random.randint(own_keys[6], (TOKENS, PICKS), 1, 65), jax.random.fold_in(own_keys[6], 1), 1, 64).astype(jnp.int32),
    }


def reference(tokens, proj_in, proj_out, expert_up, expert_down, expert_ids, weight_codes):
    codes = weight_codes.astype(jnp.float32)
    route_weights = codes / jnp.sum(codes, axis=1, keepdims=True)
    latent = lax.dot_general(tokens, proj_in, (((1,), (1,)), ((), ())), preferred_element_type=jnp.float32).astype(jnp.bfloat16)
    flat_ids = expert_ids.reshape(-1).astype(jnp.int32)
    order = jnp.argsort(flat_ids, stable=True).astype(jnp.int32)
    sorted_ids = flat_ids[order]
    source_rows = (order // PICKS).astype(jnp.int32)
    block_rows = 128
    block_count = (TOKENS * PICKS) // block_rows

    def one_block(block):
        start = (block * block_rows).astype(jnp.int32)
        ids_here = lax.dynamic_slice_in_dim(sorted_ids, start, block_rows, 0)
        rows_here = lax.dynamic_slice_in_dim(source_rows, start, block_rows, 0)
        inputs = latent[rows_here]

        def apply_one(expert, accum):
            up_here = lax.dynamic_index_in_dim(expert_up, expert, 0, keepdims=False)
            down_here = lax.dynamic_index_in_dim(expert_down, expert, 0, keepdims=False)
            hidden = jnp.dot(inputs, up_here, preferred_element_type=jnp.float32)
            hidden = jnp.square(jnp.maximum(hidden, 0.0)).astype(jnp.bfloat16)
            result = jnp.dot(hidden, down_here, preferred_element_type=jnp.float32).astype(jnp.bfloat16)
            return jnp.where((ids_here == expert)[:, None], result, accum)

        empty = jnp.zeros((block_rows, L), jnp.bfloat16)
        return lax.fori_loop(ids_here[0], ids_here[block_rows - 1] + 1, apply_one, empty)

    outputs = lax.map(one_block, jnp.arange(block_count, dtype=jnp.int32)).reshape(TOKENS * PICKS, L)
    placed = jnp.zeros((TOKENS * PICKS, L), jnp.bfloat16).at[order].set(outputs).reshape(TOKENS, PICKS, L)
    combined = jnp.sum(route_weights[:, :, None] * placed.astype(jnp.float32), axis=1).astype(jnp.bfloat16)
    return jnp.dot(combined, proj_out, preferred_element_type=jnp.float32).astype(jnp.bfloat16)
```

```python
import functools

import jax
import jax.numpy as jnp
from jax import lax
from jax.experimental import pallas as pl
from jax.experimental.pallas import tpu as pltpu
from jax.sharding import PartitionSpec as P


def expert_block(arrived, expert_up, expert_down):
    width = arrived.shape[-1]
    flat_rows = arrived.reshape(-1, width)
    hidden = jnp.dot(flat_rows, expert_up[0], preferred_element_type=jnp.float32)
    hidden = jnp.square(jnp.maximum(hidden, 0.0)).astype(jnp.bfloat16)
    result = jnp.dot(hidden, expert_down[0], preferred_element_type=jnp.float32)
    return result.astype(jnp.bfloat16).reshape(arrived.shape)


def slot_positions(bucket, live, buckets):
    labels = jnp.arange(buckets, dtype=jnp.int32)
    onehot = jnp.logical_and(bucket[:, :, None] == labels, live[:, :, None]).astype(jnp.int32)
    per_row = jnp.sum(onehot, axis=1)
    before = jnp.cumsum(per_row, axis=0) - per_row
    return jnp.take_along_axis(before, bucket, axis=1)


def per_device(tokens, proj_in, proj_out, expert_up, expert_down, expert_ids, weight_codes):
    ep_count = lax.axis_size("ep")
    group_count = lax.axis_size("grp")
    experts = ep_count * group_count
    tok_block = tokens.shape[0]
    tok_dev = tok_block // group_count
    picks = expert_ids.shape[1]
    width = expert_up.shape[1]
    capacity = max(2, (4 * tok_dev * picks + 3 * experts - 1) // (3 * experts))
    in_rows, out_rows = (
        lax.all_gather(proj_in, "ep", axis=0, tiled=True),
        lax.all_gather(proj_out, "ep", axis=0, tiled=True),
    )
    latent = lax.psum_scatter(
        lax.dot_general(
            tokens, in_rows, (((1,), (1,)), ((), ())), preferred_element_type=jnp.float32
        ),
        "grp",
        scatter_dimension=0,
        tiled=True,
    ).astype(jnp.bfloat16)
    codes = weight_codes.astype(jnp.float32)
    route_weights = codes / jnp.sum(codes, axis=1, keepdims=True)
    group_index = lax.axis_index("grp")
    my_ids = lax.dynamic_slice_in_dim(expert_ids, group_index * tok_dev, tok_dev, 0)
    my_weights = lax.dynamic_slice_in_dim(route_weights, group_index * tok_dev, tok_dev, 0)
    position = slot_positions(my_ids, jnp.ones(my_ids.shape, jnp.bool_), experts)
    spread = jnp.broadcast_to(latent[:, None, :], (tok_dev, picks, width))
    outgoing = jnp.zeros((experts, capacity, width), jnp.bfloat16).at[my_ids, position].set(spread)
    computed = expert_block(
        lax.all_to_all(outgoing, ("ep", "grp"), split_axis=0, concat_axis=0, tiled=True),
        expert_up,
        expert_down,
    )
    returned = lax.all_to_all(computed, ("ep", "grp"), split_axis=0, concat_axis=0, tiled=True)
    picked = returned[my_ids, position]
    combined = jnp.sum(my_weights[:, :, None] * picked.astype(jnp.float32), axis=1)
    latent_out = combined.astype(jnp.bfloat16)
    mixed = jnp.dot(
        lax.all_gather(latent_out, "grp", axis=0, tiled=True),
        out_rows,
        preferred_element_type=jnp.float32,
    )
    return mixed.astype(jnp.bfloat16)


MESH = pl.DeviceIdType.MESH
BF = jnp.bfloat16
F32 = jnp.float32


def nt(a, b):
    return lax.dot_general(a, b, (((1,), (1,)), ((), ())), preferred_element_type=F32)


def nn(a, b):
    return jnp.dot(a, b, preferred_element_type=F32)


SHARED = ("E1", "E2", "E3", "META", "O", "P", "Q")
OUTER = (
    ("P", 0), ("META",), ("P", 1), ("GWX", 0), ("WOUT",), ("GWX", 1), ("METAR",), ("T", 0), ("GWM", 0),
    ("Q", 0), ("Q", 1), ("T", 1), ("Q", 2), ("Q", 3), ("T", 2), ("GWM", 1), ("P", 2), ("P", 3), ("T", 3),
    ("WX",), ("T", 4), ("D", 0, 0), ("T", 5), ("D", 1, 0), ("T", 6), ("D", 2, 0), ("R", 0, 0), ("T", 7),
    ("D", 3, 0), ("WR",), ("R", 1, 0), ("T", 8), ("T", 9), ("R", 2, 0), ("T", 10), ("D", 0, 1), ("R", 3, 0),
    ("T", 11), ("D", 1, 1), ("T", 12), ("R", 0, 1), ("T", 13), ("D", 2, 1), ("E1", 0), ("T", 14), ("R", 1,
    1), ("E2", 0), ("E3", 0, 0), ("T", 15), ("D", 3, 1), ("R", 2, 1), ("E3", 0, 1), ("M", 0, 0), ("E1", 1),
    ("M", 0, 1), ("E2", 1), ("R", 3, 1), ("E3", 1, 0), ("E3", 1, 1), ("Y", 0, 0), ("M", 1, 0), ("E1", 2),
    ("M", 1, 1), ("Y", 0, 1), ("E2", 2), ("E3", 2, 0), ("Y", 1, 0), ("E3", 2, 1), ("M", 2, 0), ("Y", 1, 1),
    ("E1", 3), ("M", 2, 1), ("E2", 3), ("H", 0, 0), ("E3", 3, 0), ("H", 0, 1), ("Y", 2, 0), ("E3", 3, 1),
    ("H", 0, 2), ("M", 3, 0), ("Y", 2, 1), ("M", 3, 1), ("H", 0, 3), ("O", 0), ("H", 1, 0), ("Y", 3, 0),
    ("H", 1, 1), ("Y", 3, 1), ("H", 1, 2), ("H", 1, 3), ("O", 1), ("H", 2, 0), ("H", 2, 1), ("H", 2, 2),
    ("H", 2, 3), ("O", 2), ("H", 3, 0), ("H", 3, 1), ("H", 3, 2), ("H", 3, 3), ("O", 3),
)
INNER = (
    ("P", 0), ("META",), ("P", 1), ("F1", 0), ("GWX", 0), ("F1", 1), ("WOUT",), ("F2", 0), ("F1", 2), ("F2",
    1), ("GWX", 1), ("F1", 3), ("METAR",), ("GWM", 0), ("F2", 2), ("F1", 4), ("Q", 0), ("Q", 1), ("F2", 3),
    ("F1", 5), ("Q", 2), ("Q", 3), ("GWM", 1), ("F1", 6), ("F2", 4), ("D", 0, 0), ("P", 2), ("P", 3), ("F1",
    7), ("F2", 5), ("D", 1, 0), ("WX",), ("F2", 6), ("F1", 8), ("D", 2, 0), ("R", 0, 0), ("F1", 9), ("F2",
    7), ("D", 3, 0), ("F1", 10), ("F2", 8), ("R", 1, 0), ("F1", 11), ("F2", 9), ("R", 2, 0), ("F1", 12),
    ("F2", 10), ("D", 0, 1), ("WR",), ("F1", 13), ("F2", 11), ("D", 1, 1), ("R", 3, 0), ("F1", 14), ("F2",
    12), ("R", 0, 1), ("F1", 15), ("F2", 13), ("D", 2, 1), ("E1", 0), ("F2", 14), ("R", 1, 1), ("E2", 0),
    ("F2", 15), ("D", 3, 1), ("E3", 0, 0), ("R", 2, 1), ("E3", 0, 1), ("E1", 1), ("R", 3, 1), ("M", 0, 0),
    ("M", 0, 1), ("E2", 1), ("E3", 1, 0), ("E3", 1, 1), ("Y", 0, 0), ("M", 1, 0), ("E1", 2), ("M", 1, 1),
    ("Y", 0, 1), ("E2", 2), ("E3", 2, 0), ("Y", 1, 0), ("E3", 2, 1), ("G1", 0, 0), ("M", 2, 0), ("Y", 1, 1),
    ("G1", 0, 1), ("E1", 3), ("G1", 0, 2), ("M", 2, 1), ("G2", 0, 0), ("E2", 3), ("G1", 0, 3), ("Y", 2, 0),
    ("G2", 0, 1), ("E3", 3, 0), ("G1", 1, 0), ("G2", 0, 2), ("Y", 2, 1), ("G1", 1, 1), ("E3", 3, 1), ("G1",
    1, 2), ("G2", 0, 3), ("M", 3, 0), ("G2", 1, 0), ("O", 0), ("G1", 1, 3), ("M", 3, 1), ("G2", 1, 1),
    ("G1", 2, 0), ("G2", 1, 2), ("Y", 3, 0), ("G1", 2, 1), ("G2", 1, 3), ("O", 1), ("G1", 2, 2), ("Y", 3,
    1), ("G2", 2, 0), ("G1", 2, 3), ("G2", 2, 1), ("G1", 3, 0), ("G2", 2, 2), ("G1", 3, 1), ("G2", 2, 3),
    ("O", 2), ("G1", 3, 2), ("G2", 3, 0), ("G1", 3, 3), ("G2", 3, 1), ("G2", 3, 2), ("G2", 3, 3), ("O", 3),
)
CHUNKS = ((0, 0), (0, 1), (0, 2), (0, 3), (1, 0), (1, 1), (1, 2), (1, 3), (2, 0), (2, 1), (3, 0), (3, 1), (2, 2), (3, 2), (2, 3), (3, 3))


def segments():
    def cut(steps):
        parts = [[]]
        for step in steps:
            if step[0] in SHARED:
                parts[-1].append(step)
                parts.append([])
            else:
                parts[-1].append(step)
        return parts

    return list(zip(cut(OUTER), cut(INNER)))


def fused_kernel(
    blocks, hits, cap,
    tok, ids, codes, pin, pout, up_hbm, down_hbm, out,
    up, down, win, wout, meta, onehot_t, onehot, inv, pick, scale,
    own, s1, s2, f1, f2, lat, xs, xin, hid, ys, mates, zsum, yret, sown, s3, s4, f3, f4, ybuf,
    hbm_sem, ws, wr, os_, or_, mts, mtr, ai, bo, ra, rb, xss, xsr, ms, mr, yss, ysr, ci, co, rc, rd,
):
    rep, ep, z = lax.axis_index("rep"), lax.axis_index("ep"), lax.axis_index("grp")
    chip = ep // 2
    side = ep % 2
    mate = chip * 2 + (1 - side)
    ypart = (ep + 2) % 4
    inward = jnp.where(z < 2, z + 1, z - 1)
    outward = jnp.where(z < 2, jnp.maximum(z - 1, 0), jnp.minimum(z + 1, 3))
    inner = jnp.logical_and(z > 0, z < 3)
    outer = jnp.logical_not(inner)
    rows = tok.shape[0] // blocks
    quarter = pin.shape[0]
    half = 2 * quarter
    picks = ids.shape[1]
    pieces = ws.shape[0] // 4
    prow = quarter // 2 // pieces
    split = sown.shape[1]
    width = sown.shape[3]

    def rcopy(src, dst, s, r, **dev):
        return pltpu.make_async_remote_copy(
            src_ref=src, dst_ref=dst, send_sem=s, recv_sem=r, device_id=dev, device_id_type=MESH
        )

    loads = [
        pltpu.make_async_copy(up_hbm.at[0], up, hbm_sem.at[0]),
        pltpu.make_async_copy(down_hbm.at[0], down, hbm_sem.at[1]),
    ]

    barrier = pltpu.get_barrier_semaphore()
    for dev in ({"ep": mate}, {"ep": ypart}, {"rep": 1 - rep}, {"grp": inward}):
        pl.semaphore_signal(barrier, inc=1, device_id=dev, device_id_type=MESH)

    @pl.when(inner)
    def _():
        pl.semaphore_signal(barrier, inc=1, device_id={"grp": outward}, device_id_type=MESH)

    def gather(src, buf, at_mate, at_y, n, s, r):
        def part(which, p):
            return pl.ds(pl.multiple_of(which * (n * step) + p * step, step), step)

        step = src.shape[0] // 2 // n
        to_y, to_x, on_y, on_x = [], [], [], []
        src_slot, y_src, y_slot, relay_slot = at_mate[0], at_y[0], at_y[1], at_mate[1]
        for p in range(n):
            mine, other = part(rep, p), part(1 - rep, p)
            to_y.append(rcopy(src.at[mine], buf.at[y_src, mine], s.at[4 * p], r.at[4 * p], ep=ypart))
            to_x.append(
                rcopy(buf.at[y_slot, mine], buf.at[y_slot, mine], s.at[4 * p + 1], r.at[4 * p + 1], rep=1 - rep)
            )
            on_y.append(
                rcopy(buf.at[y_slot, mine], buf.at[relay_slot, mine], s.at[4 * p + 2], r.at[4 * p + 2], ep=mate)
            )
            on_x.append(
                rcopy(buf.at[y_slot, other], buf.at[relay_slot, other], s.at[4 * p + 3], r.at[4 * p + 3], ep=mate)
            )
        to_mate = rcopy(src, buf.at[src_slot], s.at[4 * n], r.at[4 * n], ep=mate)
        return to_mate, to_y, to_x, on_y, on_x

    win_m, win_y, win_x, win_ry, win_rx = gather(pin, win, (0, 2), (1, 1), pieces, ws, wr)
    out_m, out_y, out_x, out_ry, out_rx = gather(pout, wout, (ep, ypart), (ep, ypart), 1, os_, or_)
    meta_y = rcopy(meta.at[0], meta.at[1], mts.at[0], mtr.at[0], ep=ypart)
    meta_m = rcopy(meta.at[0], meta.at[2], mts.at[1], mtr.at[1], ep=mate)
    meta_r = rcopy(meta.at[1], meta.at[3], mts.at[2], mtr.at[2], ep=mate)

    def from_outer(k):
        return rcopy(s1.at[k], f1.at[k], ai.at[k], ra.at[k], grp=inward)

    def across(k):
        return rcopy(s1.at[k], f2.at[k], ai.at[k], rb.at[k], grp=inward)

    def to_outer(k):
        return rcopy(s2.at[k], f2.at[k], bo.at[k], rb.at[k], grp=outward)

    def keep(q, v):
        for b in range(blocks):
            own[q * blocks + b] = v[b * rows : (b + 1) * rows, :]

        @pl.when(outer)
        def _():
            for b in range(blocks):
                s1[q * blocks + b] = v[b * rows : (b + 1) * rows, :].astype(BF)

    def send_own(q):
        if q < 2:
            ready = [(q, b) for b in range(blocks)]
        else:
            ready = CHUNKS[2 * blocks :][:2] if q == 2 else CHUNKS[2 * blocks + 2 :]

        @pl.when(outer)
        def _():
            for c, b in ready:
                from_outer(c * blocks + b).start()

    def partial(q):
        w = pin[...] if q == 0 else win[q - 1]
        keep(q, nt(tok[...], w))

    for load in loads:
        load.start()
    partial(0)
    pl.semaphore_wait(barrier, jnp.where(inner, 5, 4))
    for copy in (win_m, *win_y):
        copy.start()
    send_own(0)

    def put(q, b, v):
        column = pl.multiple_of(jnp.where(q % 2 == 0, side, 1 - side) * quarter, quarter)
        lat[b, jnp.where(q < 2, chip, 1 - chip), :, pl.ds(column, quarter)] = v.astype(BF)

    def op_f1(k):
        from_outer(k).wait_recv()
        s1[k] = (own[k] + f1[k].astype(F32)).astype(BF)
        across(k).start()

    def op_f2(q, b):
        k = q * blocks + b
        across(k).wait_recv()
        v = own[k] + f2[k].astype(F32)
        s2[k] = v.astype(BF)
        to_outer(k).start()
        put(q, b, v + f1[k].astype(F32))

    def op_t(q, b):
        k = q * blocks + b
        to_outer(k).wait_recv()
        put(q, b, own[k] + f2[k].astype(F32))

    def before(n):
        i = lax.broadcasted_iota(jnp.int32, (n, n), 0)
        j = lax.broadcasted_iota(jnp.int32, (n, n), 1)
        return jnp.where(i < j, 1.0, 0.0).astype(BF)

    def placed(sel, rank, count):
        slot = lax.broadcasted_iota(jnp.int32, (count, sel.shape[1]), 0).astype(F32)
        return jnp.where(jnp.logical_and(slot == rank, sel > 0.0), 1.0, 0.0)

    def op_meta():
        i = lax.broadcasted_iota(jnp.int32, (8, picks), 0)
        j = lax.broadcasted_iota(jnp.int32, (8, picks), 1)
        pickrow = jnp.where(i == j, 1.0, 0.0).astype(BF)
        id_rows = nt(pickrow, ids[...].astype(F32).astype(BF))
        code_rows = nt(pickrow, codes[...].astype(F32).astype(BF))
        n = id_rows.shape[1]
        here = (lax.broadcasted_iota(jnp.int32, (8, n), 0) * blocks + z).astype(F32)
        table = jnp.zeros((8, n), F32)
        for p in range(picks):
            table = table + jnp.where(id_rows[p : p + 1, :] == here, code_rows[p : p + 1, :], 0.0)
        inverse = 1.0 / jnp.sum(code_rows, axis=0, keepdims=True)
        hit = jnp.where(jnp.sum(table, axis=0, keepdims=True) > 0.0, 1.0, 0.0)
        for b in range(blocks):
            at = slice(b * rows, (b + 1) * rows)
            sel = hit[:, at]
            rank = nn(jnp.broadcast_to(sel, (8, rows)).astype(BF), before(rows))[0:1, :]
            chosen = placed(sel, rank, hits)
            onehot[b] = chosen.astype(BF)
            onehot_t[b] = jnp.transpose(chosen).astype(BF)
            meta[0, b] = nt(table[:, at].astype(BF), chosen.astype(BF))
            inv[b] = jnp.transpose(jnp.broadcast_to(inverse[:, at], (rows, rows)))
        meta_y.start()
        meta_m.start()

    def op_metar():
        meta_y.wait_recv()
        meta_r.start()

    def op_q(b):
        if b == 0:
            meta_m.wait_recv()
            meta_r.wait_recv()
        for s in range(4):
            m = meta[s, b, pl.ds(ep, 1), :]
            sel = jnp.where(m > 0.0, 1.0, 0.0)
            rank = nn(jnp.broadcast_to(sel, (8, hits)).astype(BF), before(hits))[0:1, :]
            q = placed(sel, rank, cap)
            pick[b, s] = q.astype(BF)
            scale[b, s] = jnp.transpose(q * m).astype(BF)

    def x_copies(b, g):
        mine = jnp.where(g == 0, chip, 1 - chip)
        other = 1 - mine
        k = 2 * b + g
        return (
            rcopy(xs.at[b, 0, mine], xs.at[b, 1, mine], xss.at[k, 0], xsr.at[k, 0], ep=ypart),
            rcopy(xs.at[b, 0, mine], xs.at[b, 2, mine], xss.at[k, 1], xsr.at[k, 1], ep=mate),
            rcopy(xs.at[b, 1, other], xs.at[b, 3, other], xss.at[k, 2], xsr.at[k, 2], ep=mate),
        )

    def op_d(b, g):
        mine = jnp.where(g == 0, chip, 1 - chip)
        xs[b, 0, mine] = nn(onehot[b], lat[b, mine]).astype(BF)
        to_y, to_m, _ = x_copies(b, g)
        to_y.start()
        to_m.start()

    def op_r(b, g):
        to_y, _, relay = x_copies(b, g)
        to_y.wait_recv()
        relay.start()

    def op_w(b):
        for g in range(2):
            _, to_m, relay = x_copies(b, g)
            to_m.wait_recv()
            relay.wait_recv()

    cut = (hid.shape[1] // 2) // 256 * 256

    def raised(c):
        h = jnp.maximum(nn(xin[...], up[:, c]), 0.0)
        hid[:, c] = (h * h).astype(BF)

    def op_e1(b):
        op_w(b)
        if b == 0:
            for load in loads:
                load.wait()
        for s in range(4):
            for h in range(2):
                xin[s * cap : (s + 1) * cap, h * half : (h + 1) * half] = nn(
                    pick[b, s], xs[b, s, h]
                ).astype(BF)
        raised(slice(0, cut))

    def op_e2(b):
        raised(slice(cut, hid.shape[1]))

    def m_copy(b, h):
        return rcopy(ys.at[b, h, pl.ds(2, 2)], mates.at[b, h], ms.at[b, h], mr.at[b, h], ep=mate)

    def y_copy(b, h):
        return rcopy(zsum.at[b, h, 1], yret.at[b, h], yss.at[b, h], ysr.at[b, h], ep=ypart)

    def op_e3(b, h):
        o = nn(hid[...], down[:, h * half : (h + 1) * half]).astype(BF)
        for s in (2, 3, 0, 1):
            ys[b, h, s] = nn(scale[b, s], o[s * cap : (s + 1) * cap, :]).astype(BF)
        m_copy(b, h).start()

    def op_m(b, h):
        m_copy(b, h).wait_recv()
        zsum[b, h] = (ys[b, h, 0:2].astype(F32) + mates[b, h].astype(F32)).astype(BF)
        y_copy(b, h).start()

    def from_outer2(b, c):
        return rcopy(sown.at[b, c], f3.at[b, c], ci.at[b, c], rc.at[b, c], grp=inward)

    def across2(b, c):
        return rcopy(s3.at[b, c], f4.at[b, c], ci.at[b, c], rd.at[b, c], grp=inward)

    def to_outer2(b, c):
        return rcopy(s4.at[b, c], f4.at[b, c], co.at[b, c], rd.at[b, c], grp=outward)

    per_half = split // 2

    def op_y(b, h):
        y_copy(b, h).wait_recv()
        v = (zsum[b, h, 0].astype(F32) + yret[b, h].astype(F32)).astype(BF)
        v = nn(onehot_t[b], v).astype(BF)
        for i in range(per_half):
            sown[b, h * per_half + i] = v[:, i * width : (i + 1) * width]

        @pl.when(outer)
        def _():
            for i in range(per_half):
                from_outer2(b, h * per_half + i).start()

    def op_g1(b, c):
        from_outer2(b, c).wait_recv()
        s3[b, c] = (sown[b, c].astype(F32) + f3[b, c].astype(F32)).astype(BF)
        across2(b, c).start()

    def weigh(b, c, v):
        w = jnp.concatenate([inv[b]] * (width // rows), axis=1)
        ybuf[b, :, c * width : (c + 1) * width] = (v * w).astype(BF)

    def op_g2(b, c):
        across2(b, c).wait_recv()
        v = sown[b, c].astype(F32) + f4[b, c].astype(F32)
        s4[b, c] = v.astype(BF)
        to_outer2(b, c).start()
        weigh(b, c, v + f3[b, c].astype(F32))

    def op_h(b, c):
        to_outer2(b, c).wait_recv()
        weigh(b, c, sown[b, c].astype(F32) + f4[b, c].astype(F32))

    def op_o(b):
        if b == 0:
            out_m.wait_recv()
            out_ry[0].wait_recv()
            out_rx[0].wait_recv()
        full = wout[...].reshape(4 * quarter, wout.shape[2])
        out[b * rows : (b + 1) * rows, :] = nn(ybuf[b], full).astype(BF)

    def op_gwx(p):
        win_y[p].wait_recv()
        win_x[p].start()
        win_ry[p].start()

    def op_gwm(p):
        win_x[p].wait_recv()
        win_rx[p].start()

    def op_p(q):
        if q == 1:
            win_m.wait_recv()
        if q == 3:
            for p in range(pieces):
                win_ry[p].wait_recv()
                win_rx[p].wait_recv()
        partial(q)
        send_own(q)

    def op_wout():
        out_m.start()
        out_y[0].start()
        wout[ep] = pout[...]

    def op_wx():
        out_y[0].wait_recv()
        out_x[0].start()
        out_ry[0].start()

    def op_wr():
        out_x[0].wait_recv()
        out_rx[0].start()

    ops = dict(
        META=op_meta, METAR=op_metar, Q=op_q, P=op_p, D=op_d, R=op_r,
        E1=op_e1, E2=op_e2, E3=op_e3, M=op_m, Y=op_y, G1=op_g1, G2=op_g2, H=op_h, O=op_o,
        GWX=op_gwx, GWM=op_gwm, WOUT=op_wout, WX=op_wx, WR=op_wr,
        F1=lambda j: op_f1(CHUNKS[j][0] * blocks + CHUNKS[j][1]),
        F2=lambda j: op_f2(*CHUNKS[j]), T=lambda j: op_t(*CHUNKS[j]),
    )

    def steps_of(which, steps):
        if steps:
            @pl.when(which)
            def _():
                for name, *args in steps:
                    ops[name](*args)

    for at_outer, at_inner in segments():
        shared = [at_outer.pop(), at_inner.pop()] if at_outer and at_outer[-1][0] in SHARED else None
        steps_of(outer, at_outer)
        steps_of(inner, at_inner)
        if shared and shared[0] != ("P", 0):
            ops[shared[0][0]](*shared[0][1:])

    for copy in (win_m, *win_y, *win_x, *win_ry, *win_rx, out_m, *out_y, *out_x, *out_ry, *out_rx):
        copy.wait_send()
    for copy in (meta_y, meta_m, meta_r):
        copy.wait_send()
    for k in range(4 * blocks):
        from_outer(k).wait_send()
    for b in range(blocks):
        for h in range(2):
            for copy in x_copies(b, h):
                copy.wait_send()
            m_copy(b, h).wait_send()
            y_copy(b, h).wait_send()
        for c in range(split):
            from_outer2(b, c).wait_send()

    @pl.when(inner)
    def _():
        for k in range(4 * blocks):
            to_outer(k).wait_send()
        for b in range(blocks):
            for c in range(split):
                to_outer2(b, c).wait_send()


def fused_device(sizes, tokens, proj_in, proj_out, expert_up, expert_down, expert_ids, weight_codes):
    groups = sizes["grp"]
    blocks = groups
    rows = tokens.shape[0] // blocks
    picks = expert_ids.shape[1]
    experts = sizes["ep"] * groups
    hits = rows * (picks // 2) // groups
    cap = max(2, (4 * rows * picks + 3 * experts - 1) // (3 * experts))
    latent, features = proj_in.shape[0] * sizes["ep"], proj_in.shape[1]
    hidden = expert_up.shape[2]
    quarter, half = latent // 4, latent // 2
    chunks = 4 * blocks
    pieces, split = 2, 4
    wide = latent // split
    vm = pltpu.VMEM
    dma = pltpu.SemaphoreType.DMA
    scratch = [
        vm((latent, hidden), BF), vm((hidden, latent), BF),
        vm((3, *proj_in.shape), BF), vm((4, *proj_out.shape), BF),
        vm((4, blocks, 8, hits), F32), vm((blocks, rows, hits), BF), vm((blocks, hits, rows), BF),
        vm((blocks, rows, rows), F32),
        vm((blocks, 4, cap, hits), BF), vm((blocks, 4, hits, cap), BF),
        vm((chunks, rows, quarter), F32),
        *[vm((chunks, rows, quarter), BF)] * 4,
        vm((blocks, 2, rows, half), BF),
        vm((blocks, 4, 2, hits, half), BF),
        vm((4 * cap, latent), BF), vm((4 * cap, hidden), BF),
        vm((blocks, 2, 4, hits, half), BF),
        vm((blocks, 2, 2, hits, half), BF), vm((blocks, 2, 2, hits, half), BF),
        vm((blocks, 2, hits, half), BF),
        *[vm((blocks, split, rows, wide), BF)] * 5,
        vm((blocks, rows, latent), BF),
        dma((2,)), *[dma((4 * pieces + 1,))] * 2, *[dma((5,))] * 2, *[dma((3,))] * 2,
        *[dma((chunks,))] * 4,
        *[dma((2 * blocks, 3))] * 2,
        *[dma((blocks, 2))] * 4,
        *[dma((blocks, split))] * 4,
    ]
    vmem = pl.BlockSpec(memory_space=pltpu.VMEM)
    hbm = pl.BlockSpec(memory_space=pl.ANY)
    return pl.pallas_call(
        functools.partial(fused_kernel, blocks, hits, cap),
        out_shape=jax.ShapeDtypeStruct((tokens.shape[0], features), BF),
        in_specs=[vm_spec for vm_spec in [vmem] * 5] + [hbm, hbm],
        out_specs=vmem,
        scratch_shapes=scratch,
        compiler_params=pltpu.CompilerParams(
            collective_id=0, has_side_effects=True, vmem_limit_bytes=60 << 20
        ),
    )(tokens, expert_ids, weight_codes, proj_in, proj_out, expert_up, expert_down)


def solution(mesh):
    sizes = dict(mesh.shape)
    body = per_device
    if sizes["ep"] == 4 and sizes["grp"] == 4 and sizes["rep"] == 2:
        body = functools.partial(fused_device, sizes)
    in_specs = (
        P(("rep", "ep"), "grp"),
        P("ep", "grp"),
        P("ep", "grp"),
        P(("ep", "grp"), None, None),
        P(("ep", "grp"), None, None),
        P(("rep", "ep"), None),
        P(("rep", "ep"), None),
    )
    out_specs = P(("rep", "ep"), "grp")
    return jax.shard_map(
        body, mesh=mesh, in_specs=in_specs, out_specs=out_specs, check_vma=False
    )
```

```python
import functools

import jax
import jax.numpy as jnp
from jax import lax
from jax.experimental import pallas as pl
from jax.experimental.pallas import tpu as pltpu
from jax.sharding import PartitionSpec as P


def expert_block(arrived, expert_up, expert_down):
    width = arrived.shape[-1]
    flat_rows = arrived.reshape(-1, width)
    hidden = jnp.dot(flat_rows, expert_up[0], preferred_element_type=jnp.float32)
    hidden = jnp.square(jnp.maximum(hidden, 0.0)).astype(jnp.bfloat16)
    result = jnp.dot(hidden, expert_down[0], preferred_element_type=jnp.float32)
    return result.astype(jnp.bfloat16).reshape(arrived.shape)


def slot_positions(bucket, live, buckets):
    labels = jnp.arange(buckets, dtype=jnp.int32)
    onehot = jnp.logical_and(bucket[:, :, None] == labels, live[:, :, None]).astype(jnp.int32)
    per_row = jnp.sum(onehot, axis=1)
    before = jnp.cumsum(per_row, axis=0) - per_row
    return jnp.take_along_axis(before, bucket, axis=1)


def per_device(tokens, proj_in, proj_out, expert_up, expert_down, expert_ids, weight_codes):
    ep_count = lax.axis_size("ep")
    group_count = lax.axis_size("grp")
    experts = ep_count * group_count
    tok_block = tokens.shape[0]
    tok_dev = tok_block // group_count
    picks = expert_ids.shape[1]
    width = expert_up.shape[1]
    capacity = max(2, (4 * tok_dev * picks + 3 * experts - 1) // (3 * experts))
    in_rows, out_rows = (
        lax.all_gather(proj_in, "ep", axis=0, tiled=True),
        lax.all_gather(proj_out, "ep", axis=0, tiled=True),
    )
    latent = lax.psum_scatter(
        lax.dot_general(
            tokens, in_rows, (((1,), (1,)), ((), ())), preferred_element_type=jnp.float32
        ),
        "grp",
        scatter_dimension=0,
        tiled=True,
    ).astype(jnp.bfloat16)
    codes = weight_codes.astype(jnp.float32)
    route_weights = codes / jnp.sum(codes, axis=1, keepdims=True)
    group_index = lax.axis_index("grp")
    my_ids = lax.dynamic_slice_in_dim(expert_ids, group_index * tok_dev, tok_dev, 0)
    my_weights = lax.dynamic_slice_in_dim(route_weights, group_index * tok_dev, tok_dev, 0)
    position = slot_positions(my_ids, jnp.ones(my_ids.shape, jnp.bool_), experts)
    spread = jnp.broadcast_to(latent[:, None, :], (tok_dev, picks, width))
    outgoing = jnp.zeros((experts, capacity, width), jnp.bfloat16).at[my_ids, position].set(spread)
    computed = expert_block(
        lax.all_to_all(outgoing, ("ep", "grp"), split_axis=0, concat_axis=0, tiled=True),
        expert_up,
        expert_down,
    )
    returned = lax.all_to_all(computed, ("ep", "grp"), split_axis=0, concat_axis=0, tiled=True)
    picked = returned[my_ids, position]
    combined = jnp.sum(my_weights[:, :, None] * picked.astype(jnp.float32), axis=1)
    latent_out = combined.astype(jnp.bfloat16)
    mixed = jnp.dot(
        lax.all_gather(latent_out, "grp", axis=0, tiled=True),
        out_rows,
        preferred_element_type=jnp.float32,
    )
    return mixed.astype(jnp.bfloat16)


MESH = pl.DeviceIdType.MESH
BF = jnp.bfloat16
F32 = jnp.float32


def nt(a, b):
    return lax.dot_general(a, b, (((1,), (1,)), ((), ())), preferred_element_type=F32)


def nn(a, b):
    return jnp.dot(a, b, preferred_element_type=F32)


SHARED = ("E1", "E2", "E3", "META", "O", "P", "Q")
OUTER = (
    ("P", 0), ("META",), ("P", 1), ("GWX", 0), ("WOUT",), ("GWX", 1), ("GWX", 2), ("GWM", 0), ("GWX", 3),
    ("METAR",), ("GWM", 1), ("Q", 0), ("Q", 1), ("GWM", 2), ("Q", 2), ("T", 0), ("GWM", 3), ("D", 0, 0),
    ("Q", 3), ("P", 2), ("T", 1), ("D", 1, 0), ("P", 3), ("WX",), ("T", 2), ("D", 2, 0), ("R", 0, 0), ("T",
    3), ("D", 3, 0), ("R", 1, 0), ("T", 4), ("D", 0, 1), ("R", 2, 0), ("T", 5), ("D", 1, 1), ("R", 3, 0),
    ("T", 6), ("D", 2, 1), ("R", 0, 1), ("T", 7), ("D", 3, 1), ("WR",), ("R", 1, 1), ("R", 2, 1), ("T", 8),
    ("D", 0, 2), ("R", 3, 1), ("T", 9), ("D", 0, 3), ("T", 10), ("D", 1, 2), ("R", 0, 2), ("T", 11), ("D",
    1, 3), ("R", 0, 3), ("T", 12), ("D", 2, 2), ("E1", 0), ("R", 1, 2), ("T", 13), ("D", 2, 3), ("E2", 0),
    ("R", 1, 3), ("E3", 0, 0), ("T", 14), ("D", 3, 2), ("E3", 0, 1), ("R", 2, 2), ("E3", 0, 2), ("M", 0, 0),
    ("T", 15), ("D", 3, 3), ("M", 0, 1), ("E3", 0, 3), ("R", 2, 3), ("M", 0, 2), ("E1", 1), ("M", 0, 3),
    ("E2", 1), ("R", 3, 2), ("E3", 1, 0), ("Y", 0, 0), ("E3", 1, 1), ("E3", 1, 2), ("R", 3, 3), ("M", 1, 0),
    ("E3", 1, 3), ("M", 1, 1), ("E1", 2), ("M", 1, 2), ("Y", 0, 1), ("M", 1, 3), ("E2", 2), ("Y", 0, 2),
    ("E3", 2, 0), ("Y", 0, 3), ("E3", 2, 1), ("E3", 2, 2), ("M", 2, 0), ("Y", 1, 0), ("E3", 2, 3), ("M", 2,
    1), ("Y", 1, 1), ("E1", 3), ("M", 2, 2), ("M", 2, 3), ("Y", 1, 2), ("E2", 3), ("Y", 1, 3), ("E3", 3, 0),
    ("E3", 3, 1), ("Y", 2, 0), ("E3", 3, 2), ("M", 3, 0), ("E3", 3, 3), ("M", 3, 1), ("Y", 2, 1), ("M", 3,
    2), ("Y", 2, 2), ("M", 3, 3), ("H", 0, 0), ("Y", 2, 3), ("Y", 3, 0), ("H", 0, 1), ("Y", 3, 1), ("Y", 3,
    2), ("H", 0, 2), ("Y", 3, 3), ("H", 0, 3), ("O", 0), ("H", 1, 0), ("H", 1, 1), ("H", 1, 2), ("H", 1, 3),
    ("O", 1), ("H", 2, 0), ("H", 2, 1), ("H", 2, 2), ("H", 2, 3), ("O", 2), ("H", 3, 0), ("H", 3, 1), ("H",
    3, 2), ("H", 3, 3), ("O", 3),
)
INNER = (
    ("P", 0), ("META",), ("P", 1), ("GWX", 0), ("F1", 0), ("WOUT",), ("GWX", 1), ("F1", 1), ("GWX", 2),
    ("F1", 2), ("GWM", 0), ("F2", 0), ("D", 0, 0), ("GWX", 3), ("F1", 3), ("METAR",), ("GWM", 1), ("F2", 1),
    ("D", 1, 0), ("F1", 4), ("Q", 0), ("GWM", 2), ("F2", 2), ("D", 2, 0), ("F1", 5), ("Q", 1), ("GWM", 3),
    ("F2", 3), ("D", 3, 0), ("F1", 6), ("Q", 2), ("Q", 3), ("F1", 7), ("F2", 4), ("D", 0, 1), ("WX",), ("P",
    2), ("F2", 5), ("D", 1, 1), ("R", 0, 0), ("P", 3), ("R", 1, 0), ("F2", 6), ("D", 2, 1), ("R", 2, 0),
    ("F1", 8), ("F2", 7), ("D", 3, 1), ("R", 3, 0), ("F1", 9), ("R", 0, 1), ("R", 1, 1), ("F1", 10), ("R",
    2, 1), ("F2", 8), ("D", 0, 2), ("F1", 11), ("R", 3, 1), ("WR",), ("F2", 9), ("D", 0, 3), ("F1", 12),
    ("F2", 10), ("D", 1, 2), ("F1", 13), ("R", 0, 2), ("F2", 11), ("D", 1, 3), ("F1", 14), ("R", 0, 3),
    ("F2", 12), ("D", 2, 2), ("F1", 15), ("E1", 0), ("R", 1, 2), ("F2", 13), ("D", 2, 3), ("E2", 0), ("R",
    1, 3), ("E3", 0, 0), ("F2", 14), ("D", 3, 2), ("E3", 0, 1), ("R", 2, 2), ("E3", 0, 2), ("F2", 15), ("D",
    3, 3), ("M", 0, 0), ("M", 0, 1), ("E3", 0, 3), ("R", 2, 3), ("M", 0, 2), ("E1", 1), ("M", 0, 3), ("E2",
    1), ("R", 3, 2), ("E3", 1, 0), ("E3", 1, 1), ("R", 3, 3), ("E3", 1, 2), ("M", 1, 0), ("Y", 0, 0), ("E3",
    1, 3), ("M", 1, 1), ("M", 1, 2), ("Y", 0, 1), ("E1", 2), ("M", 1, 3), ("Y", 0, 2), ("E2", 2), ("Y", 0,
    3), ("E3", 2, 0), ("E3", 2, 1), ("Y", 1, 0), ("E3", 2, 2), ("M", 2, 0), ("E3", 2, 3), ("M", 2, 1), ("Y",
    1, 1), ("E1", 3), ("M", 2, 2), ("M", 2, 3), ("Y", 1, 2), ("G1", 0, 0), ("E2", 3), ("Y", 1, 3), ("E3", 3,
    0), ("E3", 3, 1), ("Y", 2, 0), ("E3", 3, 2), ("M", 3, 0), ("G1", 0, 1), ("Y", 2, 1), ("M", 3, 1), ("E3",
    3, 3), ("M", 3, 2), ("Y", 2, 2), ("G2", 0, 0), ("G1", 0, 2), ("M", 3, 3), ("Y", 2, 3), ("G1", 0, 3),
    ("Y", 3, 0), ("G2", 0, 1), ("G1", 1, 0), ("Y", 3, 1), ("G2", 0, 2), ("G1", 1, 1), ("Y", 3, 2), ("Y", 3,
    3), ("G2", 0, 3), ("G1", 1, 2), ("O", 0), ("G2", 1, 0), ("G1", 1, 3), ("G2", 1, 1), ("G1", 2, 0), ("G2",
    1, 2), ("G1", 2, 1), ("G2", 1, 3), ("G1", 2, 2), ("O", 1), ("G2", 2, 0), ("G1", 2, 3), ("G2", 2, 1),
    ("G1", 3, 0), ("G2", 2, 2), ("G1", 3, 1), ("G2", 2, 3), ("G1", 3, 2), ("O", 2), ("G2", 3, 0), ("G1", 3,
    3), ("G2", 3, 1), ("G2", 3, 2), ("G2", 3, 3), ("O", 3),
)
CHUNKS = ((0, 0), (0, 1), (0, 2), (0, 3), (1, 0), (1, 1), (1, 2), (1, 3), (2, 0), (3, 0), (2, 1), (3, 1), (2, 2), (3, 2), (2, 3), (3, 3))


def segments():
    def cut(steps):
        parts = [[]]
        for step in steps:
            if step[0] in SHARED:
                parts[-1].append(step)
                parts.append([])
            else:
                parts[-1].append(step)
        return parts

    return list(zip(cut(OUTER), cut(INNER)))


def fused_kernel(
    blocks, hits, cap,
    tok, ids, codes, pin, pout, up_hbm, down_hbm, out,
    up, down, win, wout, meta, onehot_t, onehot, inv, pick, scale,
    own, s1, s2, f1, f2, lat, xs, xin, hid, ys, mates, zsum, yret, sown, s3, s4, f3, f4, ybuf,
    hbm_sem, ws, wr, os_, or_, mts, mtr, ai, bo, ra, rb, xss, xsr, ms, mr, yss, ysr, ci, co, rc, rd,
):
    rep, ep, z = lax.axis_index("rep"), lax.axis_index("ep"), lax.axis_index("grp")
    chip = ep // 2
    mate = chip * 2 + (1 - ep % 2)
    ypart = (ep + 2) % 4
    inward = jnp.where(z < 2, z + 1, z - 1)
    outward = jnp.where(z < 2, jnp.maximum(z - 1, 0), jnp.minimum(z + 1, 3))
    inner = jnp.logical_and(z > 0, z < 3)
    outer = jnp.logical_not(inner)
    rows = tok.shape[0] // blocks
    quarter = pin.shape[0]
    picks = ids.shape[0]
    pieces = ws.shape[0] // 4
    split = sown.shape[1]
    width = sown.shape[3]

    def rcopy(src, dst, s, r, **dev):
        return pltpu.make_async_remote_copy(
            src_ref=src, dst_ref=dst, send_sem=s, recv_sem=r, device_id=dev, device_id_type=MESH
        )

    loads = [
        pltpu.make_async_copy(up_hbm.at[0], up, hbm_sem.at[0]),
        pltpu.make_async_copy(down_hbm.at[0], down, hbm_sem.at[1]),
    ]

    barrier = pltpu.get_barrier_semaphore()
    for dev in ({"ep": mate}, {"ep": ypart}, {"rep": 1 - rep}, {"grp": inward}):
        pl.semaphore_signal(barrier, inc=1, device_id=dev, device_id_type=MESH)

    @pl.when(inner)
    def _():
        pl.semaphore_signal(barrier, inc=1, device_id={"grp": outward}, device_id_type=MESH)

    def gather(src, buf, at_mate, at_y, n, s, r):
        def part(which, p):
            return pl.ds(pl.multiple_of(which * (n * step) + p * step, step), step)

        step = src.shape[0] // 2 // n
        to_y, to_x, on_y, on_x = [], [], [], []
        src_slot, y_src, y_slot, relay_slot = at_mate[0], at_y[0], at_y[1], at_mate[1]
        for p in range(n):
            mine, other = part(rep, p), part(1 - rep, p)
            to_y.append(rcopy(src.at[mine], buf.at[y_src, mine], s.at[4 * p], r.at[4 * p], ep=ypart))
            to_x.append(
                rcopy(buf.at[y_slot, mine], buf.at[y_slot, mine], s.at[4 * p + 1], r.at[4 * p + 1], rep=1 - rep)
            )
            on_y.append(
                rcopy(buf.at[y_slot, mine], buf.at[relay_slot, mine], s.at[4 * p + 2], r.at[4 * p + 2], ep=mate)
            )
            on_x.append(
                rcopy(buf.at[y_slot, other], buf.at[relay_slot, other], s.at[4 * p + 3], r.at[4 * p + 3], ep=mate)
            )
        to_mate = rcopy(src, buf.at[src_slot], s.at[4 * n], r.at[4 * n], ep=mate)
        return to_mate, to_y, to_x, on_y, on_x

    win_m, win_y, win_x, win_ry, win_rx = gather(pin, win, (0, 2), (1, 1), pieces, ws, wr)
    out_m, out_y, out_x, out_ry, out_rx = gather(pout, wout, (ep, ypart), (ep, ypart), 1, os_, or_)
    meta_y = rcopy(meta.at[0], meta.at[1], mts.at[0], mtr.at[0], ep=ypart)
    meta_m = rcopy(meta.at[0], meta.at[2], mts.at[1], mtr.at[1], ep=mate)
    meta_r = rcopy(meta.at[1], meta.at[3], mts.at[2], mtr.at[2], ep=mate)

    def from_outer(k):
        return rcopy(s1.at[k], f1.at[k], ai.at[k], ra.at[k], grp=inward)

    def across(k):
        return rcopy(s1.at[k], f2.at[k], ai.at[k], rb.at[k], grp=inward)

    def to_outer(k):
        return rcopy(s2.at[k], f2.at[k], bo.at[k], rb.at[k], grp=outward)

    def keep(q, v):
        for b in range(blocks):
            own[q * blocks + b] = v[b * rows : (b + 1) * rows, :]

        @pl.when(outer)
        def _():
            for b in range(blocks):
                s1[q * blocks + b] = v[b * rows : (b + 1) * rows, :].astype(BF)

    def send_own(q):
        if q < 2:
            ready = [(q, b) for b in range(blocks)]
        else:
            ready = CHUNKS[2 * blocks :][:1] if q == 2 else CHUNKS[2 * blocks + 1 :]

        @pl.when(outer)
        def _():
            for c, b in ready:
                from_outer(c * blocks + b).start()

    def partial(q):
        w = pin[...] if q == 0 else win[q - 1]
        keep(q, nt(tok[...], w))

    for load in loads:
        load.start()
    partial(0)
    pl.semaphore_wait(barrier, jnp.where(inner, 5, 4))
    for copy in (win_m, *win_y):
        copy.start()
    send_own(0)

    across_mate = (ypart // 2) * 2 + 1 - ypart % 2
    shards = (ep, mate, ypart, across_mate)
    arriving = (ypart, across_mate, ep, mate)

    def put(q, b, v):
        lat[b, shards[q]] = v.astype(BF)

    def op_f1(k):
        from_outer(k).wait_recv()
        s1[k] = (own[k] + f1[k].astype(F32)).astype(BF)
        across(k).start()

    def op_f2(q, b):
        k = q * blocks + b
        across(k).wait_recv()
        v = own[k] + f2[k].astype(F32)
        s2[k] = v.astype(BF)
        to_outer(k).start()
        put(q, b, v + f1[k].astype(F32))

    def op_t(q, b):
        k = q * blocks + b
        to_outer(k).wait_recv()
        put(q, b, own[k] + f2[k].astype(F32))

    def before(n):
        i = lax.broadcasted_iota(jnp.int32, (n, n), 0)
        j = lax.broadcasted_iota(jnp.int32, (n, n), 1)
        return jnp.where(i < j, 1.0, 0.0).astype(BF)

    def placed(sel, rank, count):
        slot = lax.broadcasted_iota(jnp.int32, (count, sel.shape[1]), 0).astype(F32)
        return jnp.where(jnp.logical_and(slot == rank, sel > 0.0), 1.0, 0.0)

    def op_meta():
        id_rows, code_rows = ids[...], codes[...].astype(F32)
        n = id_rows.shape[1]
        here = lax.broadcasted_iota(jnp.int32, (8, n), 0) * blocks + z
        table = jnp.zeros((8, n), F32)
        for p in range(picks):
            table = table + jnp.where(id_rows[p : p + 1, :] == here, code_rows[p : p + 1, :], 0.0)
        inverse = 1.0 / jnp.sum(code_rows, axis=0, keepdims=True)
        hit = jnp.where(jnp.sum(table, axis=0, keepdims=True) > 0.0, 1.0, 0.0)
        for b in range(blocks):
            at = slice(b * rows, (b + 1) * rows)
            sel = hit[:, at]
            rank = nn(jnp.broadcast_to(sel, (8, rows)).astype(BF), before(rows))[0:1, :]
            chosen = placed(sel, rank, hits)
            onehot[b] = chosen.astype(BF)
            onehot_t[b] = jnp.transpose(chosen).astype(BF)
            meta[0, b] = nt(table[:, at].astype(BF), chosen.astype(BF))
            inv[b] = jnp.transpose(jnp.broadcast_to(inverse[:, at], (rows, rows)))
        meta_y.start()
        meta_m.start()

    def op_metar():
        meta_y.wait_recv()
        meta_r.start()

    def op_q(b):
        if b == 0:
            meta_m.wait_recv()
            meta_r.wait_recv()
        for s in range(4):
            m = meta[s, b, pl.ds(ep, 1), :]
            sel = jnp.where(m > 0.0, 1.0, 0.0)
            rank = nn(jnp.broadcast_to(sel, (8, hits)).astype(BF), before(hits))[0:1, :]
            q = placed(sel, rank, cap)
            pick[b, s] = q.astype(BF)
            scale[b, s] = jnp.transpose(q * m).astype(BF)

    def x_copies(b, q):
        mine, other = shards[q], arriving[q]
        k = 4 * b + q
        return (
            rcopy(xs.at[b, 0, mine], xs.at[b, 1, mine], xss.at[k, 0], xsr.at[k, 0], ep=ypart),
            rcopy(xs.at[b, 0, mine], xs.at[b, 2, mine], xss.at[k, 1], xsr.at[k, 1], ep=mate),
            rcopy(xs.at[b, 1, other], xs.at[b, 3, other], xss.at[k, 2], xsr.at[k, 2], ep=mate),
        )

    def op_d(b, q):
        xs[b, 0, shards[q]] = nn(onehot[b], lat[b, shards[q]]).astype(BF)
        to_y, to_m, _ = x_copies(b, q)
        to_y.start()
        to_m.start()

    def op_r(b, q):
        to_y, _, relay = x_copies(b, q)
        to_y.wait_recv()
        relay.start()

    def op_w(b):
        for q in range(4):
            _, to_m, relay = x_copies(b, q)
            to_m.wait_recv()
            relay.wait_recv()

    cut = (hid.shape[1] // 2) // 256 * 256

    def raised(c):
        h = jnp.maximum(nn(xin[...], up[:, c]), 0.0)
        hid[:, c] = (h * h).astype(BF)

    def op_e1(b):
        op_w(b)
        if b == 0:
            for load in loads:
                load.wait()
        for s in range(4):
            for q in range(4):
                xin[s * cap : (s + 1) * cap, q * quarter : (q + 1) * quarter] = nn(
                    pick[b, s], xs[b, s, q]
                ).astype(BF)
        raised(slice(0, cut))

    def op_e2(b):
        raised(slice(cut, hid.shape[1]))

    def m_copy(b, h):
        return rcopy(ys.at[b, h, pl.ds(2, 2)], mates.at[b, h], ms.at[b, h], mr.at[b, h], ep=mate)

    def y_copy(b, h):
        return rcopy(zsum.at[b, h, 1], yret.at[b, h], yss.at[b, h], ysr.at[b, h], ep=ypart)

    def op_e3(b, h):
        o = nn(hid[...], down[:, h * width : (h + 1) * width]).astype(BF)
        for s in (2, 3, 0, 1):
            ys[b, h, s] = nn(scale[b, s], o[s * cap : (s + 1) * cap, :]).astype(BF)
        m_copy(b, h).start()

    def op_m(b, h):
        m_copy(b, h).wait_recv()
        zsum[b, h] = (ys[b, h, 0:2].astype(F32) + mates[b, h].astype(F32)).astype(BF)
        y_copy(b, h).start()

    def from_outer2(b, c):
        return rcopy(sown.at[b, c], f3.at[b, c], ci.at[b, c], rc.at[b, c], grp=inward)

    def across2(b, c):
        return rcopy(s3.at[b, c], f4.at[b, c], ci.at[b, c], rd.at[b, c], grp=inward)

    def to_outer2(b, c):
        return rcopy(s4.at[b, c], f4.at[b, c], co.at[b, c], rd.at[b, c], grp=outward)

    def op_y(b, c):
        y_copy(b, c).wait_recv()
        v = (zsum[b, c, 0].astype(F32) + yret[b, c].astype(F32)).astype(BF)
        sown[b, c] = nn(onehot_t[b], v).astype(BF)

        @pl.when(outer)
        def _():
            from_outer2(b, c).start()

    def op_g1(b, c):
        from_outer2(b, c).wait_recv()
        s3[b, c] = (sown[b, c].astype(F32) + f3[b, c].astype(F32)).astype(BF)
        across2(b, c).start()

    def weigh(b, c, v):
        w = jnp.concatenate([inv[b]] * (width // rows), axis=1)
        ybuf[b, :, c * width : (c + 1) * width] = (v * w).astype(BF)

    def op_g2(b, c):
        across2(b, c).wait_recv()
        v = sown[b, c].astype(F32) + f4[b, c].astype(F32)
        s4[b, c] = v.astype(BF)
        to_outer2(b, c).start()
        weigh(b, c, v + f3[b, c].astype(F32))

    def op_h(b, c):
        to_outer2(b, c).wait_recv()
        weigh(b, c, sown[b, c].astype(F32) + f4[b, c].astype(F32))

    def op_o(b):
        if b == 0:
            out_m.wait_recv()
            out_ry[0].wait_recv()
            out_rx[0].wait_recv()
        full = wout[...].reshape(4 * quarter, wout.shape[2])
        out[b * rows : (b + 1) * rows, :] = nn(ybuf[b], full).astype(BF)

    def op_gwx(p):
        win_y[p].wait_recv()
        win_x[p].start()
        win_ry[p].start()

    def op_gwm(p):
        win_x[p].wait_recv()
        win_rx[p].start()

    def op_p(q):
        if q == 1:
            win_m.wait_recv()
        if q == 3:
            for p in range(pieces):
                win_ry[p].wait_recv()
                win_rx[p].wait_recv()
        partial(q)
        send_own(q)

    def op_wout():
        out_m.start()
        out_y[0].start()
        wout[ep] = pout[...]

    def op_wx():
        out_y[0].wait_recv()
        out_x[0].start()
        out_ry[0].start()

    def op_wr():
        out_x[0].wait_recv()
        out_rx[0].start()

    ops = dict(
        META=op_meta, METAR=op_metar, Q=op_q, P=op_p, D=op_d, R=op_r,
        E1=op_e1, E2=op_e2, E3=op_e3, M=op_m, Y=op_y, G1=op_g1, G2=op_g2, H=op_h, O=op_o,
        GWX=op_gwx, GWM=op_gwm, WOUT=op_wout, WX=op_wx, WR=op_wr,
        F1=lambda j: op_f1(CHUNKS[j][0] * blocks + CHUNKS[j][1]),
        F2=lambda j: op_f2(*CHUNKS[j]), T=lambda j: op_t(*CHUNKS[j]),
    )

    def steps_of(which, steps):
        if steps:
            @pl.when(which)
            def _():
                for name, *args in steps:
                    ops[name](*args)

    for at_outer, at_inner in segments():
        shared = [at_outer.pop(), at_inner.pop()] if at_outer and at_outer[-1][0] in SHARED else None
        steps_of(outer, at_outer)
        steps_of(inner, at_inner)
        if shared and shared[0] != ("P", 0):
            ops[shared[0][0]](*shared[0][1:])

    for copy in (win_m, *win_y, *win_x, *win_ry, *win_rx, out_m, *out_y, *out_x, *out_ry, *out_rx):
        copy.wait_send()
    for copy in (meta_y, meta_m, meta_r):
        copy.wait_send()
    for k in range(4 * blocks):
        from_outer(k).wait_send()
    for b in range(blocks):
        for q in range(4):
            for copy in x_copies(b, q):
                copy.wait_send()
        for c in range(split):
            m_copy(b, c).wait_send()
            y_copy(b, c).wait_send()
            from_outer2(b, c).wait_send()

    @pl.when(inner)
    def _():
        for k in range(4 * blocks):
            to_outer(k).wait_send()
        for b in range(blocks):
            for c in range(split):
                to_outer2(b, c).wait_send()


def fused_device(sizes, tokens, proj_in, proj_out, expert_up, expert_down, expert_ids, weight_codes):
    groups = sizes["grp"]
    blocks = groups
    rows = tokens.shape[0] // blocks
    picks = expert_ids.shape[1]
    experts = sizes["ep"] * groups
    hits = rows * (picks // 2) // groups
    cap = max(2, (4 * rows * picks + 3 * experts - 1) // (3 * experts))
    latent, features = proj_in.shape[0] * sizes["ep"], proj_in.shape[1]
    hidden = expert_up.shape[2]
    quarter = latent // 4
    chunks = 4 * blocks
    pieces, split = 4, 4
    wide = latent // split
    vm = pltpu.VMEM
    dma = pltpu.SemaphoreType.DMA
    scratch = [
        vm((latent, hidden), BF), vm((hidden, latent), BF),
        vm((3, *proj_in.shape), BF), vm((4, *proj_out.shape), BF),
        vm((4, blocks, 8, hits), F32), vm((blocks, rows, hits), BF), vm((blocks, hits, rows), BF),
        vm((blocks, rows, rows), F32),
        vm((blocks, 4, cap, hits), BF), vm((blocks, 4, hits, cap), BF),
        vm((chunks, rows, quarter), F32),
        *[vm((chunks, rows, quarter), BF)] * 4,
        vm((blocks, 4, rows, quarter), BF),
        vm((blocks, 4, 4, hits, quarter), BF),
        vm((4 * cap, latent), BF), vm((4 * cap, hidden), BF),
        vm((blocks, split, 4, hits, wide), BF),
        vm((blocks, split, 2, hits, wide), BF), vm((blocks, split, 2, hits, wide), BF),
        vm((blocks, split, hits, wide), BF),
        *[vm((blocks, split, rows, wide), BF)] * 5,
        vm((blocks, rows, latent), BF),
        dma((2,)), *[dma((4 * pieces + 1,))] * 2, *[dma((5,))] * 2, *[dma((3,))] * 2,
        *[dma((chunks,))] * 4,
        *[dma((4 * blocks, 3))] * 2,
        *[dma((blocks, split))] * 8,
    ]
    vmem = pl.BlockSpec(memory_space=pltpu.VMEM)
    hbm = pl.BlockSpec(memory_space=pl.ANY)
    return pl.pallas_call(
        functools.partial(fused_kernel, blocks, hits, cap),
        out_shape=jax.ShapeDtypeStruct((tokens.shape[0], features), BF),
        in_specs=[vm_spec for vm_spec in [vmem] * 5] + [hbm, hbm],
        out_specs=vmem,
        scratch_shapes=scratch,
        compiler_params=pltpu.CompilerParams(
            collective_id=0, has_side_effects=True, vmem_limit_bytes=60 << 20
        ),
    )(tokens, expert_ids.T, weight_codes.T, proj_in, proj_out, expert_up, expert_down)


def solution(mesh):
    sizes = dict(mesh.shape)
    body = per_device
    if sizes["ep"] == 4 and sizes["grp"] == 4 and sizes["rep"] == 2:
        body = functools.partial(fused_device, sizes)
    in_specs = (
        P(("rep", "ep"), "grp"),
        P("ep", "grp"),
        P("ep", "grp"),
        P(("ep", "grp"), None, None),
        P(("ep", "grp"), None, None),
        P(("rep", "ep"), None),
        P(("rep", "ep"), None),
    )
    out_specs = P(("rep", "ep"), "grp")
    return jax.shard_map(
        body, mesh=mesh, in_specs=in_specs, out_specs=out_specs, check_vma=False
    )
```
